32 devices in a mesh: ens: 2 (over y), row: 4 (over z), col: 4 (over x, core).
Axes of the slice: x: 2, y: 2, z: 4, core: 2. Of those that a mesh axis runs over, the one named last changes fastest.
Arguments:
- series: float32 [24576, 256], P(('ens', 'row', 'col')), parts along dimension 0, may hold values from -22 to 22, as said below
- vectors: float32 [24576, 128], P(('ens', 'row', 'col')), parts along dimension 0, may hold values from -6 to 6
- damp_class: int32 [24576], P(('ens', 'row', 'col')), parts along dimension 0, may hold values from 0 to 15
- damp_levels: float32 [16], replicated, may hold values from 0.5 to 2
- removed_blocks: int32 [64, 32], P('ens'), parts along dimension 0, may hold values 0 or 1
Outputs:
- filtered: float32 [24576, 128], P(('ens', 'row', 'col')), parts along dimension 0
The draws below stay inside these ranges and needn't reach their ends.
There are 2 independent parts, one for each index of `ens`. The reference program is written for one: setup_inputs(seed, part) draws one part's arguments, and reference() takes and returns one part's arrays. A program takes and returns all parts, laid end to end along the dimension named above; an argument that names none is the same for every part. Nothing has to cross between parts.
Inputs may be any that keep to these rules, and one draw needn't show every extreme that they name: Each voxel's series is not constant.
All inputs are finite; a program needn't handle non-finite values.
Results may differ from the reference program's by a relative error of at most 0.0003.
Values sent between devices are 32-bit elements; how exact they have to be, the bound alone decides.
No kernel may reach another device: no remote copies, remote signals or barrier semaphores. Data moves between devices by JAX's collectives and lax.ppermute only.
A program may use at most 128 MiB of HBM per device.

```python
import math
import jax
import jax.numpy as jnp
from jax import lax

N = 12288
S = 256
K = 128
G = 384
NCLASS = 16
NBLK = 32


def draw_series(key, part):
    drawn = jnp.clip(jax.random.normal(jax.random.fold_in(key, 11), (N, S), jnp.float32), -6.0, 6.0)
    return drawn


def touch_ends(result, own_key, low, top_value):
    longest = result.shape.index(max(result.shape))
    spots = []
    for shift in (0, 1):
        where = [jax.random.randint(jax.random.fold_in(own_key, axis), (), 0, length) for axis, length in enumerate(result.shape)]
        where[longest] = (where[longest] + shift) % result.shape[longest]
        spots.append(tuple(where))
    return result.at[spots[0]].set(low).at[spots[1]].set(top_value)


def levels(key, extent, split, smallest, high):
    gain, own = 1.0, jax.random.fold_in(key, 6)
    for dim, blocks in split:
        draws = jnp.exp(jax.random.uniform(jax.random.fold_in(own, dim), (blocks,), jnp.float32, smallest / len(split), high / len(split)))
        gain = gain * jnp.repeat(draws, extent[dim] // blocks).reshape([-1 if axis == dim else 1 for axis in range(len(extent))])
    return gain


def gaussian(rng, extent, width, reach, pieces=(), held_as=jnp.bfloat16):
    level = levels(rng, extent, pieces, -0.22, 0.18) if pieces else 1.0
    array = jax.random.normal(rng, extent, jnp.float32) * width * level
    return jnp.minimum(jnp.maximum(array, -reach), reach).astype(held_as)


def setup_inputs(seed: int = 0, part: int = 0) -> dict:
    key_of = jax.random.split(jax.random.key(seed), 6)
    part_splits = jax.random.split(jax.random.fold_in(key_of[5], part), 6)
    series = draw_series(jax.random.fold_in(jax.random.fold_in(key_of[5], part), 71), part)
    vectors = gaussian(part_splits[1], (N, K), 1.0, 6.0, ((0, 16),), jnp.float32)
    damp_class = touch_ends(jax.random.randint(part_splits[2], (N,), 0, NCLASS), jax.random.fold_in(part_splits[2], 1), 0, NCLASS - 1).astype(jnp.int32)
    damp_levels = jnp.clip(jnp.exp(jax.random.uniform(key_of[3], (NCLASS,), jnp.float32, math.log(0.5), math.log(2.0))), 0.5, 2.0)
    removed_blocks = touch_ends((jax.random.randint(part_splits[4], (NBLK, NBLK), 0, 8) < 1).astype(jnp.int32), jax.random.fold_in(part_splits[4], 1), 0, 1)
    return {"series": series, "vectors": vectors, "damp_class": damp_class, "damp_levels": damp_levels, "removed_blocks": removed_blocks}


sharpness = 12.0

def standardize(series):
    centered = series - lax.optimization_barrier(jnp.mean(series, axis=1, keepdims=True))
    spread = lax.optimization_barrier(jnp.mean(centered * centered, axis=1, keepdims=True))
    return centered * lax.rsqrt(spread + 1e-05)

def reference(series, vectors, damp_class, damp_levels, removed_blocks):
    z_all = standardize(series)
    onehot = (damp_class[:, None] == jnp.arange(NCLASS, dtype=jnp.int32)[None, :]).astype(jnp.float32)
    damping = lax.optimization_barrier(jnp.sum(onehot * damp_levels[None, :], axis=1))
    keep_all = 1.0 - removed_blocks.astype(jnp.float32)
    spectral_scale = 0.5 * N * jnp.mean(damp_levels * damp_levels)

    def normal_apply(field_in):

        def block_step(running, block_index):
            offset = (block_index * G).astype(jnp.int32)
            row_series = lax.dynamic_slice_in_dim(z_all, offset, G, 0)
            row_damp = lax.dynamic_slice_in_dim(damping, offset, G, 0)
            keep_row = jnp.repeat(lax.dynamic_slice_in_dim(keep_all, block_index.astype(jnp.int32), 1, 0), G, axis=1)
            correlation = jnp.dot(row_series, z_all.T, precision=lax.Precision.HIGHEST, preferred_element_type=jnp.float32) / S
            affinity = jnp.tanh(sharpness * correlation) * keep_row * row_damp[:, None]
            partial_value = jnp.dot(affinity, field_in, precision=lax.Precision.HIGHEST, preferred_element_type=jnp.float32)
            running = running + jnp.dot(affinity.T, partial_value, precision=lax.Precision.HIGHEST, preferred_element_type=jnp.float32)
            return (running, None)
        running, _ = lax.scan(block_step, jnp.zeros((N, K), jnp.float32), jnp.arange(N // G, dtype=jnp.int32))
        return running / spectral_scale
    first_term = normal_apply(vectors) - vectors
    return 2.0 * (normal_apply(first_term) - first_term) - vectors
```

```python
import functools

import jax
import jax.numpy as jnp
from jax import lax
from jax.experimental import pallas as pl
from jax.experimental.pallas import tpu as pltpu
from jax.sharding import PartitionSpec as P

sharpness = 12.0
F32 = jnp.float32
BF16 = jnp.bfloat16


def standardize(series):
    centered = series - jnp.mean(series, axis=1, keepdims=True)
    spread = jnp.mean(centered * centered, axis=1, keepdims=True)
    return centered * lax.rsqrt(spread + 1e-05)


def damping_of(damp_class, damp_levels):
    classes = damp_levels.shape[0]
    onehot = (damp_class[:, None] == jnp.arange(classes, dtype=jnp.int32)[None, :]).astype(F32)
    return jnp.sum(onehot * damp_levels[None, :], axis=1)


def general(series, vectors, damp_class, damp_levels, removed_blocks):
    n_col = lax.axis_size("col")
    row_id = lax.axis_index("row")
    col_id = lax.axis_index("col")
    shard_rows = series.shape[0]
    samples = series.shape[1]
    total = shard_rows * n_col * lax.axis_size("row")
    z_own = standardize(series)
    damping = damping_of(damp_class, damp_levels)
    z_rows = lax.all_gather(z_own, "col", axis=0, tiled=True)
    d_rows = lax.all_gather(damping, "col", axis=0, tiled=True)
    tile_rows = z_rows.shape[0]
    blocks = removed_blocks.shape[0]
    block_size = total // blocks
    z_cols = lax.all_gather(z_own, "row", axis=0, tiled=True)
    count = z_cols.shape[0]
    row_index = row_id * tile_rows + jnp.arange(tile_rows, dtype=jnp.int32)
    position = jnp.arange(count, dtype=jnp.int32)
    col_index = ((position // shard_rows) * n_col + col_id) * shard_rows + position % shard_rows
    names = jnp.arange(blocks, dtype=jnp.int32)
    onehot_rows = (row_index[:, None] // block_size == names[None, :]).astype(F32)
    onehot_cols = (col_index[None, :] // block_size == names[:, None]).astype(F32)
    keep_rows = jnp.dot(onehot_rows, 1.0 - removed_blocks.astype(F32), preferred_element_type=F32)
    keep_full = jnp.dot(keep_rows, onehot_cols, preferred_element_type=F32)
    correlation = (
        lax.dot_general(
            z_rows,
            z_cols,
            (((1,), (1,)), ((), ())),
            precision=lax.Precision.HIGHEST,
            preferred_element_type=F32,
        )
        / samples
    )
    affinity = jnp.tanh(sharpness * correlation) * keep_full * d_rows[:, None]
    spectral_scale = 0.5 * total * jnp.mean(damp_levels * damp_levels)

    def product(field, side):
        return lax.dot_general(
            affinity,
            field,
            (((side,), (0,)), ((), ())),
            precision=lax.Precision.HIGHEST,
            preferred_element_type=F32,
        )

    def normal_apply(field_in):
        image = product(lax.all_gather(field_in, "row", axis=0, tiled=True), 1)
        image = lax.psum_scatter(image, "col", scatter_dimension=0, tiled=True)
        returned = product(lax.all_gather(image, "col", axis=0, tiled=True), 0)
        return lax.psum_scatter(returned, "row", scatter_dimension=0, tiled=True) / spectral_scale

    first_term = normal_apply(vectors) - vectors
    return 2.0 * (normal_apply(first_term) - first_term) - vectors


def split(v):
    hi = v.astype(BF16)
    return hi, (v - hi.astype(F32)).astype(BF16)


VMEM = pl.BlockSpec(memory_space=pltpu.VMEM)
SMEM = pl.BlockSpec(memory_space=pltpu.SMEM)
GRANT = 12 * 2**20


def call(kernel, name, out_shape, args, specs, scratch=(), flops=0, transcendentals=0):
    shapes = out_shape if isinstance(out_shape, tuple) else (out_shape,)
    size = sum(a.size * a.dtype.itemsize for a in (*args, *shapes))
    return pl.pallas_call(
        kernel,
        out_shape=out_shape,
        in_specs=specs,
        out_specs=tuple(VMEM for _ in shapes) if isinstance(out_shape, tuple) else VMEM,
        scratch_shapes=scratch,
        compiler_params=pltpu.CompilerParams(vmem_limit_bytes=GRANT),
        cost_estimate=pl.CostEstimate(flops=flops, bytes_accessed=size, transcendentals=transcendentals),
        name=name,
    )(*args)


def standardize_kernel(s_ref, z_ref):
    z_ref[...] = standardize(s_ref[...])


def standardize_call(series):
    return call(
        standardize_kernel, "standardize", jax.ShapeDtypeStruct(series.shape, F32), [series], [VMEM], flops=6 * series.size
    )


def build_kernel(scale, block, slot, half, ids_ref, removed_ref, zr_ref, zc0_ref, zc1_ref, th_ref, tl_ref, left, right):
    rows, samples = zr_ref.shape
    hi, lo = split(zr_ref[...])
    left[:, 0:samples] = hi
    left[:, samples : 2 * samples] = hi
    left[:, 2 * samples : 3 * samples] = lo
    for n, zc_ref in enumerate((zc0_ref, zc1_ref)):
        hi, lo = split(zc_ref[...])
        right[:, 0:samples] = hi
        right[:, samples : 2 * samples] = lo
        right[:, 2 * samples : 3 * samples] = hi
        for r in range(rows // block):
            for s in range(rows // block):
                c = lax.dot_general(
                    left[r * block : (r + 1) * block, :],
                    right[s * block : (s + 1) * block, :],
                    (((1,), (1,)), ((), ())),
                    preferred_element_type=F32,
                )
                keep = 1.0 - removed_ref[ids_ref[slot] + r, ids_ref[4 + 2 * half + n] + s].astype(F32)
                hi_t, lo_t = split(jnp.tanh(c * scale) * keep)
                to = pl.ds(n * rows + s * block, block)
                th_ref[r * block : (r + 1) * block, to] = hi_t
                tl_ref[r * block : (r + 1) * block, to] = lo_t


def build_call(slot, half, block, ids, removed, z_row, z_cols):
    rows, samples = z_row.shape
    cols = rows * len(z_cols)
    shape = jax.ShapeDtypeStruct((rows, cols), BF16)
    return call(
        functools.partial(build_kernel, sharpness / samples, block, slot, half),
        "build",
        (shape, shape),
        [ids, removed, z_row, *z_cols],
        [SMEM, SMEM, VMEM, VMEM, VMEM],
        [pltpu.VMEM((rows, 3 * samples), BF16)] * 2,
        flops=6 * rows * cols * samples,
        transcendentals=rows * cols,
    )


def forward_kernel(n_t, n_x, n_acc, *refs):
    t_refs, refs = refs[: 2 * n_t], refs[2 * n_t :]
    x_refs, refs = refs[:n_x], refs[n_x:]
    acc_refs, refs = refs[:n_acc], refs[n_acc:]
    out_refs, packed = refs[:-1], refs[-1]
    half, k = out_refs[0].shape
    at = 0
    for x_ref in x_refs:
        hi, lo = split(x_ref[...])
        packed[at : at + x_ref.shape[0], 0:k] = hi
        packed[at : at + x_ref.shape[0], k : 2 * k] = lo
        at += x_ref.shape[0]
    for n in range(n_t):
        for part in range(2):
            rows = slice(part * half, (part + 1) * half)
            wide = jnp.dot(t_refs[2 * n][rows, :], packed[...], preferred_element_type=F32)
            wide += jnp.dot(t_refs[2 * n + 1][rows, :], packed[...], preferred_element_type=F32)
            value = wide[:, 0:k] + wide[:, k : 2 * k]
            at = 2 * n + part
            out_refs[at][...] = value + acc_refs[at][...] if n_acc else value


def forward_call(tiles, xs, acc=()):
    rows, k = xs[0].shape
    depth = sum(x.shape[0] for x in xs)
    flat = [t for pair in tiles for t in pair]
    args = [*flat, *xs, *acc]
    out = jax.ShapeDtypeStruct((rows // 2, k), F32)
    return call(
        functools.partial(forward_kernel, len(tiles), len(xs), len(acc)),
        "forward",
        (out,) * (2 * len(tiles)),
        args,
        [VMEM] * len(args),
        [pltpu.VMEM((depth, 2 * k), BF16)],
        flops=8 * len(tiles) * rows * depth * k,
    )


def backward_kernel(n_t, n_y, side, has_acc, *refs):
    t_refs, refs = refs[: 2 * n_t], refs[2 * n_t :]
    y_refs, refs = refs[:n_y], refs[n_y:]
    out_ref, packed = refs[-2:]
    cols, k = out_ref.shape
    at = 0
    for y_ref in y_refs:
        hi, lo = split(y_ref[...].T)
        packed[0:k, at : at + y_ref.shape[0]] = hi
        packed[k : 2 * k, at : at + y_ref.shape[0]] = lo
        at += y_ref.shape[0]
    rows = t_refs[0].shape[0]
    wide = None
    for n, t_ref in enumerate(t_refs):
        y = packed[:, (n // 2) * rows : (n // 2 + 1) * rows]
        term = jnp.dot(y, t_ref[:, side * cols : (side + 1) * cols], preferred_element_type=F32)
        wide = term if wide is None else wide + term
    value = (wide[0:k] + wide[k : 2 * k]).T
    out_ref[...] = value + refs[0][...] if has_acc else value


def backward_call(tiles, side, ys, acc=None):
    k = ys[0].shape[1]
    depth = sum(y.shape[0] for y in ys)
    cols = tiles[0][0].shape[1] // 2
    args = [*(t for pair in tiles for t in pair), *ys, *([] if acc is None else [acc])]
    return call(
        functools.partial(backward_kernel, len(tiles), len(ys), side, acc is not None),
        "backward",
        jax.ShapeDtypeStruct((cols, k), F32),
        args,
        [VMEM] * len(args),
        [pltpu.VMEM((2 * k, depth), BF16)],
        flops=8 * cols * depth * k,
    )


def squared(series, vectors, damp_class, damp_levels, removed_blocks):
    n_row, n_col = lax.axis_size("row"), lax.axis_size("col")
    row_id, col_id = lax.axis_index("row"), lax.axis_index("col")
    rows = series.shape[0]
    total = rows * n_row * n_col
    blocks = removed_blocks.shape[0]
    block = total // blocks
    half_row, half_col = n_row // 2, n_col // 2

    def swap(flip_row, flip_col):
        pairs = [
            (r * n_col + c, (r ^ flip_row) * n_col + (c ^ flip_col)) for r in range(n_row) for c in range(n_col)
        ]
        return lambda v: lax.ppermute(v, ("row", "col"), pairs)

    far, near, side, core = swap(half_row, 0), swap(1, 0), swap(0, half_col), swap(0, 1)

    z = standardize_call(series)
    z_near = near(z)
    z_side = side(z)
    z_core = core(z)
    z_far = far(z)
    z_far_core = core(z_far)
    z_diag = side(z_near)
    v = vectors
    scale = 0.5 * total * jnp.mean(damp_levels * damp_levels)
    damping = damping_of(damp_class, damp_levels)
    weight = (damping * damping / scale)[:, None]

    slots = 4
    row_z = [z_side, z_near, z_diag, z]
    row_flips = [(0, half_col), (1, 0), (1, half_col), (0, 0)]
    col_z = [(z, z_core), (z_far, z_far_core)]
    col_flips = [(0, 0), (0, 1), (half_row, 0), (half_row, 1)]
    flips = jnp.array([f[0] for f in row_flips + col_flips]), jnp.array([f[1] for f in row_flips + col_flips])
    ids = ((row_id ^ flips[0]) * n_col + (col_id ^ flips[1])) * (rows // block)
    tile = {}
    for slot, h in ((3, 0), (0, 0), (1, 0), (3, 1), (0, 1), (1, 1), (2, 0), (2, 1)):
        tile[slot, h] = build_call(slot, h, block, ids, removed_blocks, row_z[slot], col_z[h])

    def gather(u):
        u_far = far(u)
        return (u, core(u)), (u_far, core(u_far))

    def normal_apply(field):
        mine, other = gather(field)
        early = forward_call([tile[s, 0] for s in range(slots)], mine)
        image = [None] * slots
        for s in (2, 0, 1, 3):
            image[s] = forward_call([tile[s, 1]], other, early[2 * s : 2 * s + 2])
        (sa, sb), (na, nb), (da, db), (oa, ob) = image
        q_na = na + side(da)
        q_sb = sb + near(db)
        q_oa = oa + side(sa)
        q_ob = ob + near(nb)
        half = rows // 2
        ya = (q_oa + near(q_na)) * weight[:half]
        yb = (q_ob + side(q_sb)) * weight[half:]
        y_na, y_sb = near(ya), side(yb)
        y_sa, y_nb = side(ya), near(yb)
        y_da, y_db = side(y_na), near(y_sb)
        ys = [y_sa, y_sb, y_na, y_nb, y_da, y_db]
        out = {}
        own = {}
        order = ((1, 1), (1, 0), (0, 1), (0, 0))
        for h, c in order:
            own[h, c] = backward_call([tile[3, h]], c, [ya, yb])
        for h, c in order:
            out[h, c] = backward_call([tile[s, h] for s in range(3)], c, ys, own[h, c])
        x_far = out[1, 0] + core(out[1, 1])
        x_own = out[0, 0] + core(out[0, 1])
        return x_own + far(x_far)

    first_term = normal_apply(v) - v
    return 2.0 * (normal_apply(first_term) - first_term) - v


def local(series, *rest):
    if lax.axis_size("row") == 4 and lax.axis_size("col") == 4:
        return squared(series, *rest)
    return general(series, *rest)


def solution(mesh):
    placed = (
        P(("ens", "row", "col"), None),
        P(("ens", "row", "col"), None),
        P(("ens", "row", "col")),
        P(),
        P("ens", None),
    )
    return jax.shard_map(
        local, mesh=mesh, in_specs=placed, out_specs=P(("ens", "row", "col"), None), check_vma=False
    )
```
